256 devices in a mesh: ops: 4 (over y), blk: 64 (over x, z, core).
Axes of the slice: x: 4, y: 4, z: 8, core: 2. Of those that a mesh axis runs over, the one named last changes fastest.
Arguments:
- psi: bfloat16 [16384, 8192], P('blk'), may hold values from -6 to 6
- left_env: bfloat16 [16, 64, 256, 256], P('ops', 'blk'), may hold values from -0.09375 to 0.09375
- right_env: bfloat16 [16, 64, 128, 128], P('ops', 'blk'), may hold values from -0.5 to 0.5
- left_live: int32 [64], replicated, may hold values from 64 to 256, as said below
- right_live: int32 [64], replicated, may hold values from 32 to 128, as said below
Outputs:
- hpsi: float32 [16384, 8192], P('blk', 'ops')
The draws below stay inside these ranges and needn't reach their ends.
Inputs may be any that keep to these rules, and one draw needn't show every extreme that they name: `left_live`: some left sector is fully live. `right_live`: some right sector is fully live.
All inputs are finite; a program needn't handle non-finite values.
Results may differ from the reference program's by a relative error of at most 0.0029.
Values may be sent and summed in bfloat16 or wider, within the bound.
No kernel may reach another device: no remote copies, remote signals or barrier semaphores. Data moves between devices by JAX's collectives and lax.ppermute only.
A program may use at most 128 MiB of HBM per device.

```python
import jax
import jax.numpy as jnp
from jax import lax

PL = 256
PR = 128
TERMS = 16
SECTORS = 64


def draw_left_live(key, part):
    values = jax.random.randint(key, (SECTORS,), PL // 4, PL + 1)
    where_full = jax.random.randint(jax.random.fold_in(key, 11), (), 0, SECTORS)
    return values.at[where_full].set(PL).astype(jnp.int32)


def draw_right_live(key, part):
    inner = jax.random.fold_in(key, 23)
    values = jax.random.randint(inner, (SECTORS,), PR // 4, PR + 1)
    where_full = jax.random.randint(jax.random.fold_in(key, 29), (), 0, SECTORS)
    return values.at[where_full].set(PR).astype(jnp.int32)


def shard_levels(rng, extent, shards, least, top_value):
    def one(dim, blocks):
        heights = jax.random.uniform(jax.random.fold_in(jax.random.fold_in(rng, 6), dim), (blocks,), jnp.float32, least / len(shards), top_value / len(shards))
        return jnp.repeat(jnp.exp(heights), extent[dim] // blocks).reshape((-1,) + (1,) * (len(extent) - dim - 1))

    gain = one(*shards[0])
    for cut in shards[1:]:
        gain = gain * one(*cut)
    return gain


def noise(key, extent, spread, limit, split=(), kind=jnp.bfloat16):
    drawn = spread * jax.random.normal(key, extent, jnp.float32)
    if split:
        drawn = drawn * shard_levels(key, extent, split, -0.22, 0.18)
    return jnp.clip(drawn, -limit, limit).astype(kind)


def setup_inputs(seed: int = 0) -> dict:
    streams_of = jax.random.split(jax.random.key(seed), 6)
    psi = noise(streams_of[0], (SECTORS * PL, SECTORS * PR), 1.0, 6.0, ((0, 64),))
    left_env = noise(streams_of[1], (TERMS, SECTORS, PL, PL), (PL * TERMS) ** -0.5, 0.09375, ((0, 4), (1, 64)))
    right_env = noise(streams_of[2], (TERMS, SECTORS, PR, PR), PR ** -0.5, 0.5, ((0, 4), (1, 64)))
    left_live = draw_left_live(jax.random.fold_in(streams_of[5], 71), 0)
    right_live = draw_right_live(jax.random.fold_in(streams_of[5], 71), 0)
    return {"psi": psi, "left_env": left_env, "right_env": right_env, "left_live": left_live, "right_live": right_live}


def reference(psi, left_env, right_env, left_live, right_live):
    sectors = left_live.shape[0]
    pl = left_env.shape[2]
    pr = right_env.shape[2]
    row_mask = (jnp.arange(pl, dtype=jnp.int32)[None, :] < left_live[:, None]).reshape(sectors * pl)
    col_mask = (jnp.arange(pr, dtype=jnp.int32)[None, :] < right_live[:, None]).reshape(sectors * pr)
    mask = row_mask[:, None] & col_mask[None, :]
    masked = jnp.where(mask, psi, jnp.zeros_like(psi)).astype(jnp.float32).reshape(sectors, pl, sectors, pr)

    def one_term(acc, envs):
        left_w, right_w = envs
        mixed = jnp.einsum('iab,ibjr->iajr', left_w.astype(jnp.float32), masked).astype(jnp.bfloat16)
        mixed = lax.optimization_barrier(mixed).astype(jnp.float32)
        return acc + jnp.einsum('iajr,jsr->iajs', mixed, right_w.astype(jnp.float32)), None

    start = jnp.zeros((sectors, pl, sectors, pr), jnp.float32)
    total, unused = lax.scan(one_term, start, (left_env, right_env))
    total = total.reshape(sectors * pl, sectors * pr)
    return jnp.where(mask, total, jnp.zeros_like(total))
```

```python
import functools

import jax
import jax.numpy as jnp
from jax import lax
from jax.experimental import pallas as pl
from jax.experimental.pallas import tpu as pltpu
from jax.sharding import PartitionSpec as P


X, Y, Z, C = 4, 4, 8, 2
AXES = ("ops", "blk")


def device(x, y, z, c):
    return (y % Y) * (X * Z * C) + (x % X) * (Z * C) + (z % Z) * C + (c % C)


def permute(value, move):
    pairs = []
    for y in range(Y):
        for x in range(X):
            for z in range(Z):
                for c in range(C):
                    pairs.append((device(x, y, z, c), device(*move(x, y, z, c))))
    return lax.ppermute(value, AXES, pairs)


def spread(k):
    return lambda x, y, z, c: (2 * x - y + k, x, z, c)


def along_y(d):
    return lambda x, y, z, c: (x, y - d, z, c)


def along_z(d):
    return lambda x, y, z, c: (x, y, z + d, c)


def swap_core(x, y, z, c):
    return (x, y, z, 1 - c)


def place(pos, d):
    z = ((pos[1] >> 1) + d) & (Z - 1)
    return pos[0] * Z + z, z


def piece_kernel(d, pos, left_live, right_live, psi_ref, l0, l1, l2, l3, own_ref, other_ref, *rest):
    out_ref, mixed = rest[-2], rest[-1]
    rows, width = psi_ref.shape
    half = width // 2
    terms = l0.shape[0]
    y, blk = pos[0], pos[1]
    x, core = blk >> 4, blk & 1
    sector = place(pos, d)[0] * C
    col = lax.broadcasted_iota(jnp.int32, (rows, width), 1)
    row = lax.broadcasted_iota(jnp.int32, (rows, width), 0)
    live = jnp.where(col < half, right_live[sector], right_live[sector + 1] + half)
    mask = (row < left_live[blk]) & (col < live)
    masked = jnp.where(mask, psi_ref[...], jnp.zeros((rows, width), psi_ref.dtype))
    for g, left in enumerate((l0, l1, l2, l3)):
        for t in range(terms):
            m = jnp.dot(left[t], masked, preferred_element_type=jnp.float32).astype(jnp.bfloat16)
            at = (g * terms + t) * half
            mixed[0, :, at : at + half] = m[:, :half]
            mixed[1, :, at : at + half] = m[:, half:]
    outs = []
    for which, ref in ((core, own_ref), (1 - core, other_ref)):
        rcat = jnp.concatenate(
            [ref[((x - y + g) & (X - 1)) * terms + t] for g in range(Y) for t in range(terms)],
            axis=1,
        )
        outs.append(
            lax.dot_general(
                mixed[which], rcat, (((1,), (1,)), ((), ())), preferred_element_type=jnp.float32
            )
        )
    even = jnp.where(core == 0, outs[0], outs[1])
    odd = jnp.where(core == 0, outs[1], outs[0])
    total = jnp.concatenate([even, odd], axis=1)
    out_ref[...] = jnp.where(mask, total, jnp.zeros_like(total))


def piece(d, scalars, psi, lefts, own, other, out):
    rows = psi.shape[0]
    terms = own.shape[0]
    size = own.shape[1]
    width = C * size
    columns = Z * width
    whole = lambda shape: pl.BlockSpec(shape, lambda i, *s: (0,) * len(shape))
    in_specs = [pl.BlockSpec((rows, width), lambda i, *s: (0, place(s[0], d)[0]))]
    in_specs += [whole(v.shape) for v in lefts] + [whole(own.shape), whole(other.shape)]
    args = [*scalars, psi, *lefts, own, other]
    aliases = {}
    if out is not None:
        in_specs.append(pl.BlockSpec(memory_space=pl.ANY))
        args.append(out)
        aliases = {len(args) - 1: 0}
    flops = 2 * terms * rows * width * rows + 2 * terms * rows * width * size
    return pl.pallas_call(
        functools.partial(piece_kernel, d),
        grid_spec=pltpu.PrefetchScalarGridSpec(
            num_scalar_prefetch=3,
            grid=(1,),
            in_specs=in_specs,
            out_specs=pl.BlockSpec((rows, width), lambda i, *s: (0, place(s[0], d)[1])),
            scratch_shapes=[pltpu.VMEM((2, rows, terms * size), jnp.bfloat16)],
        ),
        out_shape=jax.ShapeDtypeStruct((rows, columns), jnp.float32),
        input_output_aliases=aliases,
        cost_estimate=pl.CostEstimate(flops=flops, bytes_accessed=4 << 20, transcendentals=0),
        compiler_params=pltpu.CompilerParams(vmem_limit_bytes=24 << 20),
        name="piece",
    )(*args)


def shards(psi, left_env, right_env, left_live, right_live):
    pos = jnp.stack([lax.axis_index("ops"), lax.axis_index("blk")]).astype(jnp.int32)
    scalars = (pos, left_live, right_live)
    terms, _, size, _ = right_env.shape
    rank = left_env.shape[2]
    mine = right_env.reshape(terms, size, size)
    left = left_env.reshape(terms, rank, rank)

    groups = [permute(mine, spread(k)) for k in range(X)]
    lefts = [left] + [permute(left, along_y(d)) for d in (1, 2, 3)]
    base = jnp.concatenate(groups, axis=0)

    own = {0: base}
    for r in (1, 2, 3):
        own[-r] = permute(own[-(r - 1)], along_z(1))
        own[r] = permute(own[r - 1], along_z(-1))
    h = X * terms // 2
    own[4] = jnp.concatenate(
        [permute(own[-3][:h], along_z(1)), permute(own[3][h:], along_z(-1))], axis=0
    )
    other = {d: permute(v, swap_core) for d, v in own.items()}

    out = None
    for d in (0, 1, -1, 2, -2, 3, -3, 4):
        out = piece(d, scalars, psi, lefts, own[d], other[d], out)
    return out


def solution(mesh):
    in_specs = (P("blk", None), P("ops", "blk", None, None), P("ops", "blk", None, None), P(), P())
    out_specs = P("blk", "ops")
    return jax.shard_map(shards, mesh=mesh, in_specs=in_specs, out_specs=out_specs, check_vma=False)
```

```python
import functools

import jax
import jax.numpy as jnp
from jax import lax
from jax.experimental import pallas as pl
from jax.experimental.pallas import tpu as pltpu
from jax.sharding import PartitionSpec as P


X, Y, Z, C = 4, 4, 8, 2
AXES = ("ops", "blk")


def device(x, y, z, c):
    return (y % Y) * (X * Z * C) + (x % X) * (Z * C) + (z % Z) * C + (c % C)


def permute(value, move):
    pairs = []
    for y in range(Y):
        for x in range(X):
            for z in range(Z):
                for c in range(C):
                    pairs.append((device(x, y, z, c), device(*move(x, y, z, c))))
    return lax.ppermute(value, AXES, pairs)


def spread(k):
    return lambda x, y, z, c: (2 * x - y + k, x, z, c)


def along_y(d):
    return lambda x, y, z, c: (x, y - d * (1 - 2 * c), z, c)


def along_z(d):
    return lambda x, y, z, c: (x, y, z + d * (1 - 2 * c), c)


def swap_core(x, y, z, c):
    return (x, y, z, 1 - c)


def place(pos, e):
    z = ((pos[1] >> 1) + e * (2 * (pos[1] & 1) - 1)) & (Z - 1)
    return pos[0] * Z + z, z


def mix(d, size, left, masked_ref, out_ref):
    terms = left.shape[0]
    width = C * size
    for i in range(masked_ref.shape[1] // width):
        value = masked_ref[:, i * width : (i + 1) * width]
        for t in range(terms):
            m = jnp.dot(left[t], value, preferred_element_type=jnp.float32).astype(jnp.bfloat16)
            for p in range(C):
                out_ref[d, i * C + p, :, t * size : (t + 1) * size] = m[:, p * size : (p + 1) * size]


def first_kernel(size, pos, left_live, right_live, psi_ref, left, out_ref, masked_ref):
    rows, span = psi_ref.shape
    col = lax.broadcasted_iota(jnp.int32, (rows, size), 1)
    row_mask = lax.broadcasted_iota(jnp.int32, (rows, size), 0) < left_live[pos[1]]
    for j in range(span // size):
        at = slice(j * size, (j + 1) * size)
        mask = row_mask & (col < right_live[pos[0] * (Z * C) + j])
        value = psi_ref[:, at]
        masked_ref[:, at] = jnp.where(mask, value, jnp.zeros_like(value))
    mix(0, size, left, masked_ref, out_ref)


def next_kernel(d, size, masked_ref, left, kept, out_ref):
    mix(d, size, left, masked_ref, out_ref)


def cost(terms, rows, columns):
    flops = 2 * terms * rows * rows * columns
    return pl.CostEstimate(flops=flops, bytes_accessed=6 << 20, transcendentals=0)


def first_step(scalars, psi, left, size):
    rows = psi.shape[0]
    terms = left.shape[0]
    span = Z * C * size
    vmem = pl.BlockSpec(memory_space=pltpu.VMEM)
    return pl.pallas_call(
        functools.partial(first_kernel, size),
        grid_spec=pltpu.PrefetchScalarGridSpec(
            num_scalar_prefetch=3,
            grid=(1,),
            in_specs=[pl.BlockSpec((rows, span), lambda i, *s: (0, s[0][0])), vmem],
            out_specs=[vmem, vmem],
        ),
        out_shape=[
            jax.ShapeDtypeStruct((Y, Z * C, rows, terms * size), jnp.bfloat16),
            jax.ShapeDtypeStruct((rows, span), jnp.bfloat16),
        ],
        cost_estimate=cost(terms, rows, span),
        compiler_params=pltpu.CompilerParams(vmem_limit_bytes=8 << 20),
        name="mixed",
    )(*scalars, psi, left)


def next_step(d, masked, left, size, mixed):
    vmem = pl.BlockSpec(memory_space=pltpu.VMEM)
    return pl.pallas_call(
        functools.partial(next_kernel, d, size),
        in_specs=[vmem, vmem, vmem],
        out_specs=vmem,
        out_shape=jax.ShapeDtypeStruct(mixed.shape, mixed.dtype),
        input_output_aliases={2: 0},
        cost_estimate=cost(left.shape[0], *masked.shape),
        compiler_params=pltpu.CompilerParams(vmem_limit_bytes=8 << 20),
        name="mixed",
    )(masked, left, mixed)


def pick(values, i):
    out = values[0]
    for n, v in enumerate(values[1:], 1):
        out = jnp.where(i == n, v, out)
    return out


def total_kernel(steps, pos, left_live, right_live, mixed, *rest):
    out_ref = rest[-1]
    rows, width = out_ref.shape
    half = width // C
    y, blk = pos[0], pos[1]
    x, core = blk >> 4, blk & 1
    i = pl.program_id(0)
    there, z = place(pos, pick(steps, i))
    col = lax.broadcasted_iota(jnp.int32, (rows, half), 1)
    row = lax.broadcasted_iota(jnp.int32, (rows, half), 0)
    row_mask = row < left_live[blk]

    def one(oa, ob, pa, pb):
        for which, parts in ((core, (oa, ob)), (1 - core, (pa, pb))):
            total = None
            for k in range(X):
                ref = parts[k // 2]
                terms = ref.shape[0] // 2
                at = (k % 2) * terms
                rcat = jnp.concatenate([ref[at + t] for t in range(terms)], axis=1)
                part = lax.dot_general(
                    mixed[((y - x + k) * (1 - 2 * core)) & (Y - 1), z * C + which],
                    rcat,
                    (((1,), (1,)), ((), ())),
                    preferred_element_type=jnp.float32,
                )
                total = part if total is None else total + part
            mask = row_mask & (col < right_live[there * C + which])
            lanes = pl.ds(pl.multiple_of(which * half, half), half)
            out_ref[:, lanes] = jnp.where(mask, total, jnp.zeros_like(total))

    for n in range(len(steps)):
        pl.when(i == n)(functools.partial(one, *rest[4 * n : 4 * n + 4]))


def total_step(steps, scalars, mixed, rights, out):
    groups, _, rows, depth = mixed.shape
    size = rights[0].shape[1]
    width = C * size
    columns = Z * width
    in_specs = [pl.BlockSpec(memory_space=pltpu.VMEM)] * (1 + len(rights))
    args = [*scalars, mixed, *rights]
    aliases = {}
    if out is not None:
        in_specs.append(pl.BlockSpec(memory_space=pl.ANY))
        args.append(out)
        aliases = {len(args) - 1: 0}
    flops = 2 * groups * depth * rows * width * len(steps)
    return pl.pallas_call(
        functools.partial(total_kernel, steps),
        grid_spec=pltpu.PrefetchScalarGridSpec(
            num_scalar_prefetch=3,
            grid=(len(steps),),
            in_specs=in_specs,
            out_specs=pl.BlockSpec(
                (rows, width), lambda i, *s: (0, place(s[0], pick(steps, i))[1])
            ),
        ),
        out_shape=jax.ShapeDtypeStruct((rows, columns), jnp.float32),
        input_output_aliases=aliases,
        cost_estimate=pl.CostEstimate(flops=flops, bytes_accessed=4 << 20, transcendentals=0),
        compiler_params=pltpu.CompilerParams(vmem_limit_bytes=8 << 20),
        name="total",
    )(*args)


def body(psi, left_env, right_env, left_live, right_live):
    pos = jnp.stack([lax.axis_index("ops"), lax.axis_index("blk")]).astype(jnp.int32)
    scalars = (pos, left_live, right_live)
    terms, _, size, _ = right_env.shape
    psi = pltpu.with_memory_space_constraint(psi, pltpu.HBM)
    rank = left_env.shape[2]
    mine = right_env.reshape(terms, size, size)
    left = left_env.reshape(terms, rank, rank)

    groups = [permute(mine, spread(k)) for k in range(X)]
    lefts = {0: left, 1: permute(left, along_y(1)), 3: permute(left, along_y(-1))}
    lefts[2] = permute(lefts[1], along_y(1))

    a = {0: jnp.concatenate(groups[:2], axis=0)}
    b = {0: jnp.concatenate(groups[2:], axis=0)}
    for r in (1, 2, 3):
        for chain in (a, b):
            chain[r] = permute(chain[r - 1], along_z(1))
            chain[-r] = permute(chain[1 - r], along_z(-1))
    a[4] = permute(a[3], along_z(1))
    b[4] = permute(b[-3], along_z(-1))

    mixed, masked = first_step(scalars, psi, left, size)
    for d in (1, 3, 2):
        mixed = next_step(d, masked, lefts[d], size, mixed)
    out = None
    for steps in ((0, 1, -1), (2, -2), (3, -3), (4,)):
        rights = []
        for e in steps:
            twin = e if e in (0, 4) else -e
            rights += [a[e], b[e]]
            rights += [permute(v[twin], swap_core) for v in (a, b)]
        out = total_step(steps, scalars, mixed, rights, out)
    return out


def solution(mesh):
    in_specs = (P("blk", None), P("ops", "blk", None, None), P("ops", "blk", None, None), P(), P())
    out_specs = P("blk", "ops")
    return jax.shard_map(body, mesh=mesh, in_specs=in_specs, out_specs=out_specs, check_vma=False)
```

```python
import functools

import jax
import jax.numpy as jnp
from jax import lax
from jax.experimental import pallas as pl
from jax.experimental.pallas import tpu as pltpu
from jax.sharding import PartitionSpec as P


X, Y, Z, C = 4, 4, 8, 2
AXES = ("ops", "blk")


def device(x, y, z, c):
    return (y % Y) * (X * Z * C) + (x % X) * (Z * C) + (z % Z) * C + (c % C)


def permute(value, move):
    pairs = []
    for y in range(Y):
        for x in range(X):
            for z in range(Z):
                for c in range(C):
                    pairs.append((device(x, y, z, c), device(*move(x, y, z, c))))
    return lax.ppermute(value, AXES, pairs)


def spread(k):
    return lambda x, y, z, c: (2 * x - y + k, x, z, c)


def along_y(d):
    return lambda x, y, z, c: (x, y - d * (1 - 2 * c), z, c)


def along_z(d):
    return lambda x, y, z, c: (x, y, z + d * (1 - 2 * c), c)


def along_x(x, y, z, c):
    return (x - 1 + 2 * c, y, z, c)


def along_xz(x, y, z, c):
    return (x - 1 + 2 * c, y, z + 1 - 2 * c, c)


def swap_core(x, y, z, c):
    return (x, y, z, 1 - c)


def place(pos, e):
    z = ((pos[1] >> 1) + e * (2 * (pos[1] & 1) - 1)) & (Z - 1)
    return pos[0] * Z + z, z


def mix(d, size, left, masked_ref, out_ref):
    terms = left.shape[0]
    width = C * size
    for i in range(masked_ref.shape[1] // width):
        value = masked_ref[:, i * width : (i + 1) * width]
        for t in range(terms):
            m = jnp.dot(left[t], value, preferred_element_type=jnp.float32).astype(jnp.bfloat16)
            for p in range(C):
                out_ref[d, i * C + p, :, t * size : (t + 1) * size] = m[:, p * size : (p + 1) * size]


def first_kernel(size, pos, left_live, right_live, psi_ref, left, out_ref, masked_ref):
    rows, span = psi_ref.shape
    col = lax.broadcasted_iota(jnp.int32, (rows, size), 1)
    row_mask = lax.broadcasted_iota(jnp.int32, (rows, size), 0) < left_live[pos[1]]
    for j in range(span // size):
        at = slice(j * size, (j + 1) * size)
        mask = row_mask & (col < right_live[pos[0] * (Z * C) + j])
        value = psi_ref[:, at]
        masked_ref[:, at] = jnp.where(mask, value, jnp.zeros_like(value))
    mix(0, size, left, masked_ref, out_ref)


def next_kernel(d, size, masked_ref, left, kept, out_ref):
    mix(d, size, left, masked_ref, out_ref)


def cost(terms, rows, columns):
    flops = 2 * terms * rows * rows * columns
    return pl.CostEstimate(flops=flops, bytes_accessed=6 << 20, transcendentals=0)


def first_step(scalars, psi, left, size):
    rows = psi.shape[0]
    terms = left.shape[0]
    span = Z * C * size
    vmem = pl.BlockSpec(memory_space=pltpu.VMEM)
    return pl.pallas_call(
        functools.partial(first_kernel, size),
        grid_spec=pltpu.PrefetchScalarGridSpec(
            num_scalar_prefetch=3,
            grid=(1,),
            in_specs=[pl.BlockSpec((rows, span), lambda i, *s: (0, s[0][0])), vmem],
            out_specs=[vmem, vmem],
        ),
        out_shape=[
            jax.ShapeDtypeStruct((Y, Z * C, rows, terms * size), jnp.bfloat16),
            jax.ShapeDtypeStruct((rows, span), jnp.bfloat16),
        ],
        cost_estimate=cost(terms, rows, span),
        compiler_params=pltpu.CompilerParams(vmem_limit_bytes=8 << 20),
        name="mixed",
    )(*scalars, psi, left)


def next_step(d, masked, left, size, mixed):
    vmem = pl.BlockSpec(memory_space=pltpu.VMEM)
    return pl.pallas_call(
        functools.partial(next_kernel, d, size),
        in_specs=[vmem, vmem, vmem],
        out_specs=vmem,
        out_shape=jax.ShapeDtypeStruct(mixed.shape, mixed.dtype),
        input_output_aliases={2: 0},
        cost_estimate=cost(left.shape[0], *masked.shape),
        compiler_params=pltpu.CompilerParams(vmem_limit_bytes=8 << 20),
        name="mixed",
    )(masked, left, mixed)


def pick(values, i):
    out = values[0]
    for n, v in enumerate(values[1:], 1):
        out = jnp.where(i == n, v, out)
    return out


def total_kernel(steps, pos, left_live, right_live, mixed, *rest):
    out_ref = rest[-1]
    rows, width = out_ref.shape
    half = width // C
    y, blk = pos[0], pos[1]
    x, core = blk >> 4, blk & 1
    i = pl.program_id(0)
    there, z = place(pos, pick(steps, i))
    col = lax.broadcasted_iota(jnp.int32, (rows, half), 1)
    row = lax.broadcasted_iota(jnp.int32, (rows, half), 0)
    row_mask = row < left_live[blk]

    def one(oa, ob, pa, pb):
        for which, parts in ((core, (oa, ob)), (1 - core, (pa, pb))):
            total = None
            for n in range(X):
                ref, h = parts[n // 2], n % 2
                k = 2 * h + 1 if n < 2 else 2 * h + 2 * which
                terms = ref.shape[0] // 2
                rcat = jnp.concatenate([ref[h * terms + t] for t in range(terms)], axis=1)
                part = lax.dot_general(
                    mixed[((y - x + k) * (1 - 2 * core)) & (Y - 1), z * C + which],
                    rcat,
                    (((1,), (1,)), ((), ())),
                    preferred_element_type=jnp.float32,
                )
                total = part if total is None else total + part
            mask = row_mask & (col < right_live[there * C + which])
            lanes = pl.ds(pl.multiple_of(which * half, half), half)
            out_ref[:, lanes] = jnp.where(mask, total, jnp.zeros_like(total))

    for n in range(len(steps)):
        pl.when(i == n)(functools.partial(one, *rest[4 * n : 4 * n + 4]))


def total_step(steps, scalars, mixed, rights, out):
    groups, _, rows, depth = mixed.shape
    size = rights[0].shape[1]
    width = C * size
    columns = Z * width
    in_specs = [pl.BlockSpec(memory_space=pltpu.VMEM)] * (1 + len(rights))
    args = [*scalars, mixed, *rights]
    aliases = {}
    if out is not None:
        in_specs.append(pl.BlockSpec(memory_space=pl.ANY))
        args.append(out)
        aliases = {len(args) - 1: 0}
    flops = 2 * groups * depth * rows * width * len(steps)
    return pl.pallas_call(
        functools.partial(total_kernel, steps),
        grid_spec=pltpu.PrefetchScalarGridSpec(
            num_scalar_prefetch=3,
            grid=(len(steps),),
            in_specs=in_specs,
            out_specs=pl.BlockSpec(
                (rows, width), lambda i, *s: (0, place(s[0], pick(steps, i))[1])
            ),
        ),
        out_shape=jax.ShapeDtypeStruct((rows, columns), jnp.float32),
        input_output_aliases=aliases,
        cost_estimate=pl.CostEstimate(flops=flops, bytes_accessed=4 << 20, transcendentals=0),
        compiler_params=pltpu.CompilerParams(vmem_limit_bytes=8 << 20),
        name="total",
    )(*args)


def body(psi, left_env, right_env, left_live, right_live):
    pos = jnp.stack([lax.axis_index("ops"), lax.axis_index("blk")]).astype(jnp.int32)
    scalars = (pos, left_live, right_live)
    terms, _, size, _ = right_env.shape
    psi = pltpu.with_memory_space_constraint(psi, pltpu.HBM)
    rank = left_env.shape[2]
    mine = right_env.reshape(terms, size, size)
    left = left_env.reshape(terms, rank, rank)

    groups = [permute(mine, spread(k)) for k in (1, 3)]
    lefts = {0: left, 1: permute(left, along_y(1)), 3: permute(left, along_y(-1))}
    lefts[2] = permute(lefts[1], along_y(1))

    a = {0: jnp.concatenate(groups, axis=0)}
    for r in (1, 2, 3, 4):
        a[r] = permute(a[r - 1], along_z(1))
        if r < 4:
            a[-r] = permute(a[1 - r], along_z(-1))
    b = {e: permute(a[e], along_x) for e in a if e < 4}
    b[4] = permute(a[3], along_xz)

    mixed, masked = first_step(scalars, psi, left, size)
    for d in (1, 3, 2):
        mixed = next_step(d, masked, lefts[d], size, mixed)
    out = None
    for steps in ((0, 1, -1), (2, -2), (3, -3, 4)):
        rights = []
        for e in steps:
            twin = e if e in (0, 4) else -e
            rights += [a[e], b[e]]
            rights += [permute(v[twin], swap_core) for v in (a, b)]
        out = total_step(steps, scalars, mixed, rights, out)
    return out


def solution(mesh):
    in_specs = (P("blk", None), P("ops", "blk", None, None), P("ops", "blk", None, None), P(), P())
    out_specs = P("blk", "ops")
    return jax.shard_map(body, mesh=mesh, in_specs=in_specs, out_specs=out_specs, check_vma=False)
```
